32 devices in a mesh: pts: 32 (over z, y, x, core).
Axes of the slice: x: 2, y: 2, z: 4, core: 2. Of those that a mesh axis runs over, the one named last changes fastest.
Arguments:
- features: float32 [65536, 128], P('pts'), may hold values from -6 to 6
- factor: float32 [65536, 1024], P('pts'), may hold values from -0.375 to 0.375
- targets: float32 [65536, 256], P('pts'), may hold values from -6 to 6
- pivots: int32 [4, 256], replicated, may hold values from 0 to 65535, as said below
Outputs:
- residuals: float32 [65536, 256], P('pts')
- scores: float32 [4, 256, 256], replicated
The draws below stay inside these ranges and needn't reach their ends.
Inputs may be any that keep to these rules, and one draw needn't show every extreme that they name: Owners of pivots are uneven: low point indices are picked more often. Indices may repeat.
All inputs are finite; a program needn't handle non-finite values.
Results may differ from the reference program's by a relative error of at most 0.0003.
Values sent between devices are 32-bit elements; how exact they have to be, the bound alone decides.
A program may use at most 192 MiB of HBM per device.

```python
import jax
import jax.numpy as jnp
from jax import lax

FEATS = 128
RANK = 1024
TARGETS = 256
PIV = 256
BLOCKS = 4
NPTS = 65536


def draw_pivots(key, part):
    first, second = jax.random.split(jax.random.fold_in(key, 17))
    one = jax.random.randint(first, (BLOCKS, PIV), 0, NPTS)
    two = jax.random.randint(second, (BLOCKS, PIV), 0, NPTS)
    picked = jnp.minimum(one, two).astype(jnp.int32)
    picked = picked.at[0, 0].set(0)
    picked = picked.at[0, 1].set(NPTS - 1)
    return picked


def block_levels(rng, shape, shards, low, largest):
    factor_of, own = 1.0, jax.random.fold_in(rng, 6)
    for axis_at, blocks in shards:
        heights = jnp.exp(jax.random.uniform(jax.random.fold_in(own, axis_at), (blocks,), jnp.float32, low / len(shards), largest / len(shards)))
        factor_of = factor_of * jnp.repeat(heights, shape[axis_at] // blocks).reshape([-1 if axis == axis_at else 1 for axis in range(len(shape))])
    return factor_of


def noise(own_key, extent, width, most, shards=(), held_as=jnp.bfloat16):
    factor_of = block_levels(own_key, extent, shards, -0.22, 0.18) if shards else 1.0
    drawn = jax.random.normal(own_key, extent, jnp.float32) * width * factor_of
    return jnp.minimum(jnp.maximum(drawn, -most), most).astype(held_as)


def setup_inputs(seed: int = 0) -> dict:
    streams_of = jax.random.split(jax.random.key(seed), 5)
    return {
        "features": noise(streams_of[0], (NPTS, FEATS), 1.0, 6.0, ((0, 32),), jnp.float32),
        "factor": noise(streams_of[1], (NPTS, RANK), (RANK // 4) ** -0.5, 0.375, ((0, 32),), jnp.float32),
        "targets": noise(streams_of[2], (NPTS, TARGETS), 1.0, 6.0, ((0, 32),), jnp.float32),
        "pivots": draw_pivots(jax.random.fold_in(streams_of[4], 71), 0),
    }


def kernel_cols(points, pivot_feats):
    left = lax.optimization_barrier(jnp.sum(points * points, axis=1))[:, None]
    right = lax.optimization_barrier(jnp.sum(pivot_feats * pivot_feats, axis=1))[None, :]
    cross = jnp.dot(points.astype(jnp.float32), pivot_feats.T.astype(jnp.float32), precision=lax.Precision.HIGHEST, preferred_element_type=jnp.float32)
    return jnp.exp(-(left + right - 2.0 * cross) * (0.5 / FEATS))

def hdot(a, b):
    return jnp.dot(a.astype(jnp.float32), b.astype(jnp.float32), precision=lax.Precision.HIGHEST, preferred_element_type=jnp.float32)

def reference(features, factor, targets, pivots):
    resid = targets
    extras = []
    score_list = []
    eye = jnp.eye(PIV, dtype=jnp.float32)
    for block in range(BLOCKS):
        idx = pivots[block]
        cols = kernel_cols(features, features[idx]) - hdot(factor, factor[idx].T)
        for extra in extras:
            cols = cols - hdot(extra, extra[idx].T)
        gram = hdot(cols.T, cols)
        lower = jnp.linalg.cholesky(gram / NPTS + 0.05 * eye)
        normed = lax.linalg.triangular_solve(lower, cols, left_side=False, lower=True, transpose_a=True)
        qq = hdot(normed.T, normed)
        qy = hdot(normed.T, resid)
        ridge = jnp.linalg.cholesky(qq / NPTS + 0.1 * eye)
        middle = lax.linalg.triangular_solve(ridge, qy / NPTS, left_side=True, lower=True)
        beta = lax.linalg.triangular_solve(ridge, middle, left_side=True, lower=True, transpose_a=True)
        resid = resid - hdot(normed, beta)
        score_list.append(qy / jnp.sqrt(jnp.float32(NPTS)))
        extras.append(normed * (1.0 / jnp.sqrt(jnp.float32(PIV))))
    return (resid, jnp.stack(score_list))
```

```python
import jax
import jax.numpy as jnp
from jax import lax
from jax.sharding import PartitionSpec as P

LOAD = 0.05
RIDGE = 0.1


def dot(a, b, precision=lax.Precision.HIGH):
    return jnp.dot(a, b, precision=precision, preferred_element_type=jnp.float32)


def dot_tn(a, b, precision=lax.Precision.HIGH):
    return lax.dot_general(
        a, b, (((0,), (0,)), ((), ())), precision=precision, preferred_element_type=jnp.float32
    )


def dot_nt(a, b, precision=lax.Precision.HIGH):
    return lax.dot_general(
        a, b, (((1,), (1,)), ((), ())), precision=precision, preferred_element_type=jnp.float32
    )


def fdot(a, b):
    return dot(a, b, lax.Precision.HIGHEST)


def fdot_tn(a, b):
    return dot_tn(a, b, lax.Precision.HIGHEST)


def fdot_nt(a, b):
    return dot_nt(a, b, lax.Precision.HIGHEST)


def raw_cols(points, rows, pivot_feats, pivot_rows):
    left = jnp.sum(points * points, axis=1)[:, None]
    right = jnp.sum(pivot_feats * pivot_feats, axis=1)[None, :]
    cross = dot_nt(points, pivot_feats)
    scale = 0.5 / points.shape[1]
    return jnp.exp(-(left + right - 2.0 * cross) * scale) - dot_nt(rows, pivot_rows)


def owned_rows(table, index_list, offset, count):
    local = index_list - offset
    owned = (local >= 0) & (local < count)
    safe = jnp.clip(local, 0, count - 1)
    return jnp.take(table, safe, axis=0) * owned[:, None].astype(table.dtype)


def ridge_inverse(inv_lower):
    eye = jnp.eye(inv_lower.shape[0], dtype=jnp.float32)
    mat = (1.0 + RIDGE) * eye - LOAD * fdot_nt(inv_lower, inv_lower)
    first = 2.0 / (1.0 + 2.0 * RIDGE)
    err = first * (1.0 + RIDGE) - 1.0
    scale = 2.0 / (2.0 - err * err)
    est = scale * first * (2.0 * eye - first * mat)
    err = scale - 1.0
    while err > 1e-8:
        scale = 2.0 / (2.0 - err * err)
        est = scale * fdot(est, 2.0 * eye - fdot(mat, est))
        err = scale - 1.0
    return est


def factor_inverse(mat):
    lower = jnp.linalg.cholesky(mat)
    eye = jnp.eye(mat.shape[0], dtype=jnp.float32)
    return lax.linalg.triangular_solve(lower, eye, left_side=True, lower=True)


def chain(grams, at_pivots, blocks, piv, npts):
    eye = jnp.eye(piv, dtype=jnp.float32)
    scores, steps = [], []
    for c in range(blocks):
        own, rest = grams[c][:, :piv], grams[c][:, piv:]
        inv_lower = factor_inverse(own / npts + LOAD * eye)
        product = fdot(inv_lower, rest[:, (blocks - 1 - c) * piv :])
        scores.append(product * (1.0 / npts**0.5))
        beta = fdot(ridge_inverse(inv_lower), product * (1.0 / npts))
        width = (blocks - 1 - c) * piv
        if width:
            seen = at_pivots[c]
            coeff = fdot_tn(inv_lower, jnp.concatenate([fdot_nt(inv_lower, seen) * (1.0 / piv), beta], 1))
            after = rest - fdot(own, coeff)
            for b in range(c + 1, blocks):
                lo = (b - c - 1) * piv
                grams[b] = (
                    grams[b]
                    - fdot_tn(rest[:, lo : lo + piv], coeff[:, lo:])
                    - fdot_tn(coeff[:, lo : lo + piv], after[:, lo:])
                )
            for d in range(c + 1, blocks - 1):
                lo = (d - c - 1) * piv
                at_pivots[d] = at_pivots[d] - fdot(seen[lo + piv :], coeff[:, lo : lo + piv])
        else:
            coeff = fdot_tn(inv_lower, beta)
        steps.append(coeff)
    weights = [None] * blocks
    for c in reversed(range(blocks)):
        own = steps[c][:, (blocks - 1 - c) * piv :]
        if c < blocks - 1:
            own = own - fdot(steps[c][:, : (blocks - 1 - c) * piv], jnp.concatenate(weights[c + 1 :], 0))
        weights[c] = own
    return jnp.concatenate(weights, 0), scores


def per_device(features, factor, targets, pivots):
    count = features.shape[0]
    blocks, piv = pivots.shape
    npts = count * lax.axis_size("pts")
    offset = lax.axis_index("pts") * count
    idx = pivots.reshape(-1)
    piv_feats, piv_rows = lax.psum(
        (owned_rows(features, idx, offset, count), owned_rows(factor, idx, offset, count)), "pts"
    )
    cols = raw_cols(features, factor, piv_feats, piv_rows)
    joined = jnp.concatenate([cols, targets], axis=1)
    grams = lax.psum(
        [dot_tn(cols[:, c * piv : (c + 1) * piv], joined[:, c * piv :]) for c in range(blocks)], "pts"
    )
    at_pivots = [
        raw_cols(
            piv_feats[(c + 1) * piv :],
            piv_rows[(c + 1) * piv :],
            piv_feats[c * piv : (c + 1) * piv],
            piv_rows[c * piv : (c + 1) * piv],
        )
        for c in range(blocks - 1)
    ]
    weights, scores = chain(list(grams), at_pivots, blocks, piv, npts)
    return targets - dot(cols, weights), jnp.stack(scores)


def solution(mesh):
    in_specs = (P("pts", None), P("pts", None), P("pts", None), P())
    out_specs = (P("pts", None), P())
    return jax.shard_map(
        per_device, mesh=mesh, in_specs=in_specs, out_specs=out_specs, check_vma=False
    )
```

```python
import jax
import jax.numpy as jnp
from jax import lax
from jax.experimental import pallas as pl
from jax.experimental.pallas import tpu as pltpu
from jax.sharding import PartitionSpec as P

LOAD = 0.05
RIDGE = 0.1
PANEL = 64
GROUP = 4


def dot(a, b, precision=lax.Precision.HIGH):
    return jnp.dot(a, b, precision=precision, preferred_element_type=jnp.float32)


def dot_tn(a, b, precision=lax.Precision.HIGH):
    return lax.dot_general(
        a, b, (((0,), (0,)), ((), ())), precision=precision, preferred_element_type=jnp.float32
    )


def dot_nt(a, b, precision=lax.Precision.HIGH):
    return lax.dot_general(
        a, b, (((1,), (1,)), ((), ())), precision=precision, preferred_element_type=jnp.float32
    )


def fdot(a, b):
    return dot(a, b, lax.Precision.HIGHEST)


def fdot_tn(a, b):
    return dot_tn(a, b, lax.Precision.HIGHEST)


def fdot_nt(a, b):
    return dot_nt(a, b, lax.Precision.HIGHEST)


def raw_cols(points, rows, pivot_feats, pivot_rows):
    left = jnp.sum(points * points, axis=1)[:, None]
    right = jnp.sum(pivot_feats * pivot_feats, axis=1)[None, :]
    cross = dot_nt(points, pivot_feats)
    scale = 0.5 / points.shape[1]
    return jnp.exp(-(left + right - 2.0 * cross) * scale) - dot_nt(rows, pivot_rows)


def owned_rows(table, index_list, offset, count):
    local = index_list - offset
    owned = (local >= 0) & (local < count)
    safe = jnp.clip(local, 0, count - 1)
    return jnp.take(table, safe, axis=0) * owned[:, None].astype(table.dtype)


def ridge_inverse(inv_lower):
    eye = jnp.eye(inv_lower.shape[0], dtype=jnp.float32)
    mat = (1.0 + RIDGE) * eye - LOAD * fdot_nt(inv_lower, inv_lower)
    first = 2.0 / (1.0 + 2.0 * RIDGE)
    err = first * (1.0 + RIDGE) - 1.0
    scale = 2.0 / (2.0 - err * err)
    est = scale * first * (2.0 * eye - first * mat)
    err = scale - 1.0
    while err > 1e-8:
        scale = 2.0 / (2.0 - err * err)
        est = scale * fdot(est, 2.0 * eye - fdot(mat, est))
        err = scale - 1.0
    return est


def panel_inverse(mat):
    n = mat.shape[0]
    row_id = lax.broadcasted_iota(jnp.int32, (n, 2 * n), 0)
    lane_id = lax.broadcasted_iota(jnp.int32, (n, 2 * n), 1)
    eye = (row_id == lane_id - n).astype(jnp.float32)
    work = jnp.concatenate([mat, eye[:, n:]], axis=1)
    for start in range(0, n, GROUP):
        heads = [
            jnp.broadcast_to(work[:, start + q : start + q + 1], (n, 2 * n)) for q in range(GROUP)
        ]
        for q in range(GROUP):
            k = start + q
            mult = jnp.where(row_id > k, heads[q] * (1.0 / heads[q][k : k + 1, :]), 0.0)
            for p in range(q + 1, GROUP):
                heads[p] = heads[p] - mult * heads[p][k : k + 1, :]
            work = work - mult * work[k : k + 1, :]
    diag = jnp.sum(jnp.where(row_id == lane_id, work, 0.0), axis=1, keepdims=True)
    return work[:, n:] * (1.0 / jnp.sqrt(diag))


def inverse_lower(mat):
    n = mat.shape[0]
    if n <= PANEL:
        return panel_inverse(mat)
    h = n // 2
    top = inverse_lower(mat[:h, :h])
    side = fdot_nt(mat[h:, :h], top)
    bottom = inverse_lower(mat[h:, h:] - fdot_nt(side, side))
    corner = -fdot(bottom, fdot(side, top))
    upper = jnp.concatenate([top, jnp.zeros((h, h), jnp.float32)], axis=1)
    return jnp.concatenate([upper, jnp.concatenate([corner, bottom], axis=1)], axis=0)


def factor_kernel(mat_ref, out_ref):
    out_ref[...] = inverse_lower(mat_ref[...])


def factor_inverse(mat):
    return pl.pallas_call(
        factor_kernel,
        out_shape=jax.ShapeDtypeStruct(mat.shape, jnp.float32),
        in_specs=[pl.BlockSpec(memory_space=pltpu.VMEM)],
        out_specs=pl.BlockSpec(memory_space=pltpu.VMEM),
    )(mat)


def chain(grams, at_pivots, blocks, piv, npts):
    eye = jnp.eye(piv, dtype=jnp.float32)
    scores, steps = [], []
    for c in range(blocks):
        own, rest = grams[c][:, :piv], grams[c][:, piv:]
        inv_lower = factor_inverse(own / npts + LOAD * eye)
        product = fdot(inv_lower, rest[:, (blocks - 1 - c) * piv :])
        scores.append(product * (1.0 / npts**0.5))
        beta = fdot(ridge_inverse(inv_lower), product * (1.0 / npts))
        width = (blocks - 1 - c) * piv
        if width:
            seen = at_pivots[c]
            coeff = fdot_tn(inv_lower, jnp.concatenate([fdot_nt(inv_lower, seen) * (1.0 / piv), beta], 1))
            after = rest - fdot(own, coeff)
            for b in range(c + 1, blocks):
                lo = (b - c - 1) * piv
                grams[b] = (
                    grams[b]
                    - fdot_tn(rest[:, lo : lo + piv], coeff[:, lo:])
                    - fdot_tn(coeff[:, lo : lo + piv], after[:, lo:])
                )
            for d in range(c + 1, blocks - 1):
                lo = (d - c - 1) * piv
                at_pivots[d] = at_pivots[d] - fdot(seen[lo + piv :], coeff[:, lo : lo + piv])
        else:
            coeff = fdot_tn(inv_lower, beta)
        steps.append(coeff)
    weights = [None] * blocks
    for c in reversed(range(blocks)):
        own = steps[c][:, (blocks - 1 - c) * piv :]
        if c < blocks - 1:
            own = own - fdot(steps[c][:, : (blocks - 1 - c) * piv], jnp.concatenate(weights[c + 1 :], 0))
        weights[c] = own
    return jnp.concatenate(weights, 0), scores


def per_device(features, factor, targets, pivots):
    count = features.shape[0]
    blocks, piv = pivots.shape
    npts = count * lax.axis_size("pts")
    offset = lax.axis_index("pts") * count
    idx = pivots.reshape(-1)
    piv_feats, piv_rows = lax.psum(
        (owned_rows(features, idx, offset, count), owned_rows(factor, idx, offset, count)), "pts"
    )
    cols = raw_cols(features, factor, piv_feats, piv_rows)
    joined = jnp.concatenate([cols, targets], axis=1)
    grams = lax.psum(
        [dot_tn(cols[:, c * piv : (c + 1) * piv], joined[:, c * piv :]) for c in range(blocks)], "pts"
    )
    at_pivots = [
        raw_cols(
            piv_feats[(c + 1) * piv :],
            piv_rows[(c + 1) * piv :],
            piv_feats[c * piv : (c + 1) * piv],
            piv_rows[c * piv : (c + 1) * piv],
        )
        for c in range(blocks - 1)
    ]
    weights, scores = chain(list(grams), at_pivots, blocks, piv, npts)
    return targets - dot(cols, weights), jnp.stack(scores)


def solution(mesh):
    in_specs = (P("pts", None), P("pts", None), P("pts", None), P())
    out_specs = (P("pts", None), P())
    return jax.shard_map(
        per_device, mesh=mesh, in_specs=in_specs, out_specs=out_specs, check_vma=False
    )
```

```python
import functools

import jax
import jax.numpy as jnp
from jax import lax
from jax.experimental import pallas as pl
from jax.experimental.pallas import tpu as pltpu
from jax.sharding import PartitionSpec as P

LOAD = 0.05
RIDGE = 0.1
PANEL = 64
GROUP = 4


def dot(a, b, precision=lax.Precision.HIGH):
    return jnp.dot(a, b, precision=precision, preferred_element_type=jnp.float32)


def dot_tn(a, b, precision=lax.Precision.HIGH):
    return lax.dot_general(
        a, b, (((0,), (0,)), ((), ())), precision=precision, preferred_element_type=jnp.float32
    )


def dot_nt(a, b, precision=lax.Precision.HIGH):
    return lax.dot_general(
        a, b, (((1,), (1,)), ((), ())), precision=precision, preferred_element_type=jnp.float32
    )


def fdot(a, b):
    return dot(a, b, lax.Precision.HIGHEST)


def fdot_tn(a, b):
    return dot_tn(a, b, lax.Precision.HIGHEST)


def fdot_nt(a, b):
    return dot_nt(a, b, lax.Precision.HIGHEST)


def raw_cols(points, rows, pivot_feats, pivot_rows):
    left = jnp.sum(points * points, axis=1)[:, None]
    right = jnp.sum(pivot_feats * pivot_feats, axis=1)[None, :]
    cross = dot_nt(points, pivot_feats)
    scale = 0.5 / points.shape[1]
    return jnp.exp(-(left + right - 2.0 * cross) * scale) - dot_nt(rows, pivot_rows)


def owned_rows(table, index_list, offset, count):
    local = index_list - offset
    owned = (local >= 0) & (local < count)
    safe = jnp.clip(local, 0, count - 1)
    return jnp.take(table, safe, axis=0) * owned[:, None].astype(table.dtype)


def ridge_inverse(inv_lower):
    eye = jnp.eye(inv_lower.shape[0], dtype=jnp.float32)
    mat = (1.0 + RIDGE) * eye - LOAD * fdot_nt(inv_lower, inv_lower)
    first = 2.0 / (1.0 + 2.0 * RIDGE)
    err = first * (1.0 + RIDGE) - 1.0
    scale = 2.0 / (2.0 - err * err)
    est = scale * first * (2.0 * eye - first * mat)
    err = scale - 1.0
    while err > 1e-8:
        scale = 2.0 / (2.0 - err * err)
        est = scale * fdot(est, 2.0 * eye - fdot(mat, est))
        err = scale - 1.0
    return est


def panel_inverse(mat):
    n = mat.shape[0]
    row_id = lax.broadcasted_iota(jnp.int32, (n, 2 * n), 0)
    lane_id = lax.broadcasted_iota(jnp.int32, (n, 2 * n), 1)
    eye = (row_id == lane_id - n).astype(jnp.float32)
    work = jnp.concatenate([mat, eye[:, n:]], axis=1)
    for start in range(0, n, GROUP):
        heads = [
            jnp.broadcast_to(work[:, start + q : start + q + 1], (n, 2 * n)) for q in range(GROUP)
        ]
        for q in range(GROUP):
            k = start + q
            mult = jnp.where(row_id > k, heads[q] * (1.0 / heads[q][k : k + 1, :]), 0.0)
            for p in range(q + 1, GROUP):
                heads[p] = heads[p] - mult * heads[p][k : k + 1, :]
            work = work - mult * work[k : k + 1, :]
    diag = jnp.sum(jnp.where(row_id == lane_id, work, 0.0), axis=1, keepdims=True)
    return work[:, n:] * (1.0 / jnp.sqrt(diag))


def inverse_lower(mat):
    n = mat.shape[0]
    if n <= PANEL:
        return panel_inverse(mat)
    h = n // 2
    top = inverse_lower(mat[:h, :h])
    side = fdot_nt(mat[h:, :h], top)
    bottom = inverse_lower(mat[h:, h:] - fdot_nt(side, side))
    corner = -fdot(bottom, fdot(side, top))
    upper = jnp.concatenate([top, jnp.zeros((h, h), jnp.float32)], axis=1)
    return jnp.concatenate([upper, jnp.concatenate([corner, bottom], axis=1)], axis=0)


def factor_kernel(mat_ref, out_ref):
    out_ref[...] = inverse_lower(mat_ref[...])


def factor_inverse(mat):
    return pl.pallas_call(
        factor_kernel,
        out_shape=jax.ShapeDtypeStruct(mat.shape, jnp.float32),
        in_specs=[pl.BlockSpec(memory_space=pltpu.VMEM)],
        out_specs=pl.BlockSpec(memory_space=pltpu.VMEM),
    )(mat)


def chain(grams, at_pivots, blocks, piv, npts):
    eye = jnp.eye(piv, dtype=jnp.float32)
    scores, steps = [], []
    for c in range(blocks):
        own, rest = grams[c][:, :piv], grams[c][:, piv:]
        inv_lower = factor_inverse(own / npts + LOAD * eye)
        product = fdot(inv_lower, rest[:, (blocks - 1 - c) * piv :])
        scores.append(product * (1.0 / npts**0.5))
        beta = fdot(ridge_inverse(inv_lower), product * (1.0 / npts))
        width = (blocks - 1 - c) * piv
        if width:
            seen = at_pivots[c]
            coeff = fdot_tn(inv_lower, jnp.concatenate([fdot_nt(inv_lower, seen) * (1.0 / piv), beta], 1))
            after = rest - fdot(own, coeff)
            for b in range(c + 1, blocks):
                lo = (b - c - 1) * piv
                grams[b] = (
                    grams[b]
                    - fdot_tn(rest[:, lo : lo + piv], coeff[:, lo:])
                    - fdot_tn(coeff[:, lo : lo + piv], after[:, lo:])
                )
            for d in range(c + 1, blocks - 1):
                lo = (d - c - 1) * piv
                at_pivots[d] = at_pivots[d] - fdot(seen[lo + piv :], coeff[:, lo : lo + piv])
        else:
            coeff = fdot_tn(inv_lower, beta)
        steps.append(coeff)
    weights = [None] * blocks
    for c in reversed(range(blocks)):
        own = steps[c][:, (blocks - 1 - c) * piv :]
        if c < blocks - 1:
            own = own - fdot(steps[c][:, : (blocks - 1 - c) * piv], jnp.concatenate(weights[c + 1 :], 0))
        weights[c] = own
    return jnp.concatenate(weights, 0), scores


def reduce_kernel(devices, widths, in_ref, out_ref, acc, got, full, send_sem, recv_sem):
    me = lax.axis_index("pts")
    rows = in_ref.shape[0]
    bits = devices.bit_length() - 1
    turn = max(1, (bits - 1) // 3)
    rest = list(range(1, bits))
    parts, lane = [], 0
    for p, width in enumerate(widths):
        shift = (p * turn) % max(1, len(rest))
        parts.append(([0] + rest[shift:] + rest[:shift], pl.ds(lane, width)))
        lane += width

    def side_of(bit):
        return lax.rem(me // (1 << bit), 2)

    def partner_of(bit):
        return me + (1 - 2 * side_of(bit)) * (1 << bit)

    def copy(src, dst, slot, p, bit):
        return pltpu.make_async_remote_copy(
            src_ref=src,
            dst_ref=dst,
            send_sem=send_sem.at[slot, p],
            recv_sem=recv_sem.at[slot, p],
            device_id=(partner_of(bit),),
            device_id_type=pl.DeviceIdType.MESH,
        )

    barrier = pltpu.get_barrier_semaphore()
    for bit in range(bits):
        pl.semaphore_signal(
            barrier, inc=1, device_id=(partner_of(bit),), device_id_type=pl.DeviceIdType.MESH
        )
    pl.semaphore_wait(barrier, bits)

    offs = [me * 0 for _ in parts]
    for s in range(bits):
        half = rows >> (s + 1)
        base = rows - 2 * half
        held = in_ref if s == 0 else acc
        copies, keeps = [], []
        for p, (order, lanes) in enumerate(parts):
            side = side_of(order[s])
            give = pl.ds(pl.multiple_of(offs[p] + (1 - side) * half, 8), half)
            offs[p] = offs[p] + side * half
            keeps.append(pl.ds(pl.multiple_of(offs[p], 8), half))
            copies.append(copy(held.at[give, lanes], got.at[pl.ds(base, half), lanes], s, p, order[s]))
            copies[-1].start()
        last = s == bits - 1
        for p, (order, lanes) in enumerate(parts):
            copies[p].wait()
            total = held[keeps[p], lanes] + got[pl.ds(base, half), lanes]
            if last:
                full[keeps[p], lanes] = total
            else:
                acc[keeps[p], lanes] = total
    for s in reversed(range(bits)):
        half = rows >> (s + 1)
        copies = []
        for p, (order, lanes) in enumerate(parts):
            have = pl.ds(pl.multiple_of(offs[p], 8), half)
            copies.append(copy(full.at[have, lanes], full.at[have, lanes], 2 * bits - 1 - s, p, order[s]))
            copies[-1].start()
            offs[p] = offs[p] - side_of(order[s]) * half
        for one in copies:
            one.wait()
    out_ref[...] = full[...]


def all_sum(array, widths, collective_id):
    devices = lax.axis_size("pts")
    slots = 2 * (devices.bit_length() - 1)
    return pl.pallas_call(
        functools.partial(reduce_kernel, devices, widths),
        out_shape=jax.ShapeDtypeStruct(array.shape, jnp.float32),
        in_specs=[pl.BlockSpec(memory_space=pltpu.VMEM)],
        out_specs=pl.BlockSpec(memory_space=pltpu.VMEM),
        scratch_shapes=[
            pltpu.VMEM(array.shape, jnp.float32),
            pltpu.VMEM(array.shape, jnp.float32),
            pltpu.VMEM(array.shape, jnp.float32),
            pltpu.SemaphoreType.DMA((slots, len(widths))),
            pltpu.SemaphoreType.DMA((slots, len(widths))),
        ],
        compiler_params=pltpu.CompilerParams(
            collective_id=collective_id, has_side_effects=True, vmem_limit_bytes=40 << 20
        ),
    )(array)


def lane_thirds(width):
    tiles = width // 128
    return tuple(128 * ((tiles + p) // 3) for p in (2, 1, 0))


def sum_grams(grams):
    first = jnp.concatenate([grams[0], grams[3]], axis=1)
    second = jnp.concatenate([grams[1], grams[2]], axis=1)
    half = first.shape[1] // 2
    packed = jnp.concatenate(
        [first[:, :half], first[:, half:], second[:, :half], second[:, half:]], axis=0
    )
    packed = all_sum(packed, lane_thirds(half), 1)
    piv = first.shape[0]
    q = [packed[i * piv : (i + 1) * piv] for i in range(4)]
    first = jnp.concatenate(q[:2], axis=1)
    second = jnp.concatenate(q[2:], axis=1)
    w0, w1 = grams[0].shape[1], grams[1].shape[1]
    return [first[:, :w0], second[:, :w1], second[:, w1:], first[:, w0:]]


def per_device(features, factor, targets, pivots):
    count = features.shape[0]
    blocks, piv = pivots.shape
    npts = count * lax.axis_size("pts")
    offset = lax.axis_index("pts") * count
    idx = pivots.reshape(-1)
    picked = jnp.concatenate(
        [owned_rows(features, idx, offset, count), owned_rows(factor, idx, offset, count)], axis=1
    )
    picked = all_sum(picked, lane_thirds(picked.shape[1]), 0)
    piv_feats, piv_rows = picked[:, : features.shape[1]], picked[:, features.shape[1] :]
    cols = raw_cols(features, factor, piv_feats, piv_rows)
    joined = jnp.concatenate([cols, targets], axis=1)
    grams = sum_grams(
        [dot_tn(cols[:, c * piv : (c + 1) * piv], joined[:, c * piv :]) for c in range(blocks)]
    )
    at_pivots = [
        raw_cols(
            piv_feats[(c + 1) * piv :],
            piv_rows[(c + 1) * piv :],
            piv_feats[c * piv : (c + 1) * piv],
            piv_rows[c * piv : (c + 1) * piv],
        )
        for c in range(blocks - 1)
    ]
    weights, scores = chain(list(grams), at_pivots, blocks, piv, npts)
    return targets - dot(cols, weights), jnp.stack(scores)


def solution(mesh):
    in_specs = (P("pts", None), P("pts", None), P("pts", None), P())
    out_specs = (P("pts", None), P())
    return jax.shard_map(
        per_device, mesh=mesh, in_specs=in_specs, out_specs=out_specs, check_vma=False
    )
```

```python
import functools

import jax
import jax.numpy as jnp
from jax import lax
from jax.experimental import pallas as pl
from jax.experimental.pallas import tpu as pltpu
from jax.sharding import PartitionSpec as P

LOAD = 0.05
RIDGE = 0.1
PANEL = 64
GROUP = 8


def dot(a, b, precision=lax.Precision.HIGH):
    return jnp.dot(a, b, precision=precision, preferred_element_type=jnp.float32)


def dot_tn(a, b, precision=lax.Precision.HIGH):
    return lax.dot_general(
        a, b, (((0,), (0,)), ((), ())), precision=precision, preferred_element_type=jnp.float32
    )


def dot_nt(a, b, precision=lax.Precision.HIGH):
    return lax.dot_general(
        a, b, (((1,), (1,)), ((), ())), precision=precision, preferred_element_type=jnp.float32
    )


def fdot(a, b):
    return dot(a, b, lax.Precision.HIGHEST)


def fdot_tn(a, b):
    return dot_tn(a, b, lax.Precision.HIGHEST)


def fdot_nt(a, b):
    return dot_nt(a, b, lax.Precision.HIGHEST)


def raw_cols(points, rows, pivot_feats, pivot_rows):
    left = jnp.sum(points * points, axis=1)[:, None]
    right = jnp.sum(pivot_feats * pivot_feats, axis=1)[None, :]
    cross = dot_nt(points, pivot_feats)
    scale = 0.5 / points.shape[1]
    return jnp.exp(-(left + right - 2.0 * cross) * scale) - dot_nt(rows, pivot_rows)


def owned_rows(table, index_list, offset, count):
    local = index_list - offset
    owned = (local >= 0) & (local < count)
    safe = jnp.clip(local, 0, count - 1)
    return jnp.take(table, safe, axis=0) * owned[:, None].astype(table.dtype)


def ridge_inverse(inv_lower):
    eye = jnp.eye(inv_lower.shape[0], dtype=jnp.float32)
    mat = (1.0 + RIDGE) * eye - LOAD * fdot_nt(inv_lower, inv_lower)
    first = 2.0 / (1.0 + 2.0 * RIDGE)
    err = first * (1.0 + RIDGE) - 1.0
    scale = 2.0 / (2.0 - err * err)
    est = scale * first * (2.0 * eye - first * mat)
    err = scale - 1.0
    while err > 1e-8:
        scale = 2.0 / (2.0 - err * err)
        mul = fdot if err * err < 1e-7 else dot
        est = scale * mul(est, 2.0 * eye - mul(mat, est))
        err = scale - 1.0
    return est


def panel_inverse(mat):
    n = mat.shape[0]
    row_id = lax.broadcasted_iota(jnp.int32, (n, 2 * n), 0)
    lane_id = lax.broadcasted_iota(jnp.int32, (n, 2 * n), 1)
    eye = (row_id == lane_id - n).astype(jnp.float32)
    work = jnp.concatenate([mat, eye[:, n:]], axis=1)
    for start in range(0, n, GROUP):
        heads = [
            jnp.broadcast_to(work[:, start + q : start + q + 1], (n, 2 * n)) for q in range(GROUP)
        ]
        for q in range(GROUP):
            k = start + q
            mult = jnp.where(row_id > k, heads[q] * (1.0 / heads[q][k : k + 1, :]), 0.0)
            for p in range(q + 1, GROUP):
                heads[p] = heads[p] - mult * heads[p][k : k + 1, :]
            work = work - mult * work[k : k + 1, :]
    diag = jnp.sum(jnp.where(row_id == lane_id, work, 0.0), axis=1, keepdims=True)
    return work[:, n:] * (1.0 / jnp.sqrt(diag))


def inverse_lower(mat):
    n = mat.shape[0]
    if n <= PANEL:
        return panel_inverse(mat)
    h = n // 2
    top = inverse_lower(mat[:h, :h])
    side = fdot_nt(mat[h:, :h], top)
    bottom = inverse_lower(mat[h:, h:] - fdot_nt(side, side))
    corner = -fdot(bottom, fdot(side, top))
    upper = jnp.concatenate([top, jnp.zeros((h, h), jnp.float32)], axis=1)
    return jnp.concatenate([upper, jnp.concatenate([corner, bottom], axis=1)], axis=0)


def factor_kernel(mat_ref, out_ref):
    out_ref[...] = inverse_lower(mat_ref[...])


def factor_inverse(mat):
    return pl.pallas_call(
        factor_kernel,
        out_shape=jax.ShapeDtypeStruct(mat.shape, jnp.float32),
        in_specs=[pl.BlockSpec(memory_space=pltpu.VMEM)],
        out_specs=pl.BlockSpec(memory_space=pltpu.VMEM),
    )(mat)


def chain(grams, at_pivots, blocks, piv, npts):
    eye = jnp.eye(piv, dtype=jnp.float32)
    scores, steps = [], []
    for c in range(blocks):
        own, rest = grams[c][:, :piv], grams[c][:, piv:]
        inv_lower = factor_inverse(own / npts + LOAD * eye)
        product = fdot(inv_lower, rest[:, (blocks - 1 - c) * piv :])
        scores.append(product * (1.0 / npts**0.5))
        beta = fdot(ridge_inverse(inv_lower), product * (1.0 / npts))
        width = (blocks - 1 - c) * piv
        if width:
            seen = at_pivots[c]
            coeff = fdot_tn(inv_lower, jnp.concatenate([fdot_nt(inv_lower, seen) * (1.0 / piv), beta], 1))
            after = rest - fdot(own, coeff)
            for b in range(c + 1, blocks):
                lo = (b - c - 1) * piv
                grams[b] = (
                    grams[b]
                    - fdot_tn(rest[:, lo : lo + piv], coeff[:, lo:])
                    - fdot_tn(coeff[:, lo : lo + piv], after[:, lo:])
                )
            for d in range(c + 1, blocks - 1):
                lo = (d - c - 1) * piv
                at_pivots[d] = at_pivots[d] - fdot(seen[lo + piv :], coeff[:, lo : lo + piv])
        else:
            coeff = fdot_tn(inv_lower, beta)
        steps.append(coeff)
    weights = [None] * blocks
    for c in reversed(range(blocks)):
        own = steps[c][:, (blocks - 1 - c) * piv :]
        if c < blocks - 1:
            own = own - fdot(steps[c][:, : (blocks - 1 - c) * piv], jnp.concatenate(weights[c + 1 :], 0))
        weights[c] = own
    return jnp.concatenate(weights, 0), scores


def reduce_kernel(devices, widths, in_ref, out_ref, acc, got, full, send_sem, recv_sem):
    me = lax.axis_index("pts")
    rows = in_ref.shape[0]
    bits = devices.bit_length() - 1
    turn = max(1, (bits - 1) // 3)
    rest = list(range(1, bits))
    parts, lane = [], 0
    for p, width in enumerate(widths):
        shift = (p * turn) % max(1, len(rest))
        parts.append(([0] + rest[shift:] + rest[:shift], pl.ds(lane, width)))
        lane += width

    def side_of(bit):
        return lax.rem(me // (1 << bit), 2)

    def partner_of(bit):
        return me + (1 - 2 * side_of(bit)) * (1 << bit)

    def copy(src, dst, slot, p, bit):
        return pltpu.make_async_remote_copy(
            src_ref=src,
            dst_ref=dst,
            send_sem=send_sem.at[slot, p],
            recv_sem=recv_sem.at[slot, p],
            device_id=(partner_of(bit),),
            device_id_type=pl.DeviceIdType.MESH,
        )

    barrier = pltpu.get_barrier_semaphore()
    for bit in range(bits):
        pl.semaphore_signal(
            barrier, inc=1, device_id=(partner_of(bit),), device_id_type=pl.DeviceIdType.MESH
        )
    pl.semaphore_wait(barrier, bits)

    offs = [me * 0 for _ in parts]
    for s in range(bits):
        half = rows >> (s + 1)
        base = rows - 2 * half
        held = in_ref if s == 0 else acc
        copies, keeps = [], []
        for p, (order, lanes) in enumerate(parts):
            side = side_of(order[s])
            give = pl.ds(pl.multiple_of(offs[p] + (1 - side) * half, 8), half)
            offs[p] = offs[p] + side * half
            keeps.append(pl.ds(pl.multiple_of(offs[p], 8), half))
            copies.append(copy(held.at[give, lanes], got.at[pl.ds(base, half), lanes], s, p, order[s]))
            copies[-1].start()
        last = s == bits - 1
        for p, (order, lanes) in enumerate(parts):
            copies[p].wait()
            total = held[keeps[p], lanes] + got[pl.ds(base, half), lanes]
            if last:
                full[keeps[p], lanes] = total
            else:
                acc[keeps[p], lanes] = total
    for s in reversed(range(bits)):
        half = rows >> (s + 1)
        copies = []
        for p, (order, lanes) in enumerate(parts):
            have = pl.ds(pl.multiple_of(offs[p], 8), half)
            copies.append(copy(full.at[have, lanes], full.at[have, lanes], 2 * bits - 1 - s, p, order[s]))
            copies[-1].start()
            offs[p] = offs[p] - side_of(order[s]) * half
        for one in copies:
            one.wait()
    out_ref[...] = full[...]


def all_sum(array, widths, collective_id):
    devices = lax.axis_size("pts")
    slots = 2 * (devices.bit_length() - 1)
    return pl.pallas_call(
        functools.partial(reduce_kernel, devices, widths),
        out_shape=jax.ShapeDtypeStruct(array.shape, jnp.float32),
        in_specs=[pl.BlockSpec(memory_space=pltpu.VMEM)],
        out_specs=pl.BlockSpec(memory_space=pltpu.VMEM),
        scratch_shapes=[
            pltpu.VMEM(array.shape, jnp.float32),
            pltpu.VMEM(array.shape, jnp.float32),
            pltpu.VMEM(array.shape, jnp.float32),
            pltpu.SemaphoreType.DMA((slots, len(widths))),
            pltpu.SemaphoreType.DMA((slots, len(widths))),
        ],
        compiler_params=pltpu.CompilerParams(
            collective_id=collective_id, has_side_effects=True, vmem_limit_bytes=40 << 20
        ),
    )(array)


def lane_thirds(width):
    tiles = width // 128
    return tuple(128 * ((tiles + p) // 3) for p in (2, 1, 0))


def sum_grams(grams):
    first = jnp.concatenate([grams[0], grams[3]], axis=1)
    second = jnp.concatenate([grams[1], grams[2]], axis=1)
    half = first.shape[1] // 2
    packed = jnp.concatenate(
        [first[:, :half], first[:, half:], second[:, :half], second[:, half:]], axis=0
    )
    packed = all_sum(packed, lane_thirds(half), 1)
    piv = first.shape[0]
    q = [packed[i * piv : (i + 1) * piv] for i in range(4)]
    first = jnp.concatenate(q[:2], axis=1)
    second = jnp.concatenate(q[2:], axis=1)
    w0, w1 = grams[0].shape[1], grams[1].shape[1]
    return [first[:, :w0], second[:, :w1], second[:, w1:], first[:, w0:]]


def per_device(features, factor, targets, pivots):
    count = features.shape[0]
    blocks, piv = pivots.shape
    npts = count * lax.axis_size("pts")
    offset = lax.axis_index("pts") * count
    idx = pivots.reshape(-1)
    picked = jnp.concatenate(
        [owned_rows(features, idx, offset, count), owned_rows(factor, idx, offset, count)], axis=1
    )
    picked = all_sum(picked, lane_thirds(picked.shape[1]), 0)
    piv_feats, piv_rows = picked[:, : features.shape[1]], picked[:, features.shape[1] :]
    cols = raw_cols(features, factor, piv_feats, piv_rows)
    joined = jnp.concatenate([cols, targets], axis=1)
    grams = sum_grams(
        [dot_tn(cols[:, c * piv : (c + 1) * piv], joined[:, c * piv :]) for c in range(blocks)]
    )
    at_pivots = [
        raw_cols(
            piv_feats[(c + 1) * piv :],
            piv_rows[(c + 1) * piv :],
            piv_feats[c * piv : (c + 1) * piv],
            piv_rows[c * piv : (c + 1) * piv],
        )
        for c in range(blocks - 1)
    ]
    weights, scores = chain(list(grams), at_pivots, blocks, piv, npts)
    return targets - dot(cols, weights), jnp.stack(scores)


def solution(mesh):
    in_specs = (P("pts", None), P("pts", None), P("pts", None), P())
    out_specs = (P("pts", None), P())
    return jax.shard_map(
        per_device, mesh=mesh, in_specs=in_specs, out_specs=out_specs, check_vma=False
    )
```
